32 devices in a mesh: lines: 2 (over x), tile: 16 (over z, y, core).
Axes of the slice: x: 2, y: 2, z: 4, core: 2. Of those that a mesh axis runs over, the one named last changes fastest.
Arguments:
- traces: bfloat16 [1024, 512, 512], P(('lines', 'tile')), parts along dimension 0, may hold values from -6 to 6
Outputs:
- multiples: bfloat16 [1024, 512, 512], P(('lines', 'tile')), parts along dimension 0
The draws below stay inside these ranges and needn't reach their ends.
There are 2 independent parts, one for each index of `lines`. The reference program is written for one: setup_inputs(seed, part) draws one part's arguments, and reference() takes and returns one part's arrays. A program takes and returns all parts, laid end to end along the dimension named above; each array names one. Nothing has to cross between parts.
All inputs are finite; a program needn't handle non-finite values.
Results may differ from the reference program's by a relative error of at most 0.011.
Values may be sent and summed in bfloat16 or wider, within the bound.
No kernel may reach another device: no remote copies, remote signals or barrier semaphores. Data moves between devices by JAX's collectives and lax.ppermute only.
A program may use at most 128 MiB of HBM per device.

```python
import math
import jax
import jax.numpy as jnp
from jax import lax

S = 512
NT = 512
F = 128


def level_of(rng, dims, shards, smallest, high):
    gain, own = 1.0, jax.random.fold_in(rng, 6)
    for dim, shards_of in shards:
        heights = jnp.exp(jax.random.uniform(jax.random.fold_in(own, dim), (shards_of,), jnp.float32, smallest / len(shards), high / len(shards)))
        gain = gain * jnp.repeat(heights, dims[dim] // shards_of).reshape([-1 if axis == dim else 1 for axis in range(len(dims))])
    return gain


def gaussian(own_key, extent, spread, reach, split=(), kind=jnp.bfloat16):
    entries = jax.random.normal(own_key, extent, jnp.float32) * spread
    if len(split) > 0:
        entries = level_of(own_key, extent, split, -0.22, 0.18) * entries
    return jnp.clip(entries, min=-reach, max=reach).astype(kind)


def setup_inputs(seed: int = 0, part: int = 0) -> dict:
    keys = jax.random.split(jax.random.key(seed), 2)
    part_splits = jax.random.split(jax.random.fold_in(keys[1], part), 2)
    return {
        "traces": gaussian(part_splits[0], (S, S, NT), 1.0, 6.0, ((0, 16),)),
    }


def make_tables():
    times = jnp.arange(NT, dtype=jnp.int32)
    freqs = jnp.arange(F, dtype=jnp.int32)
    phase = times[:, None] * freqs[None, :] % NT
    angle = phase.astype(jnp.float32) * (2.0 * math.pi / NT)
    norm = 1.0 / math.sqrt(NT)
    forward = jnp.stack([jnp.cos(angle), -jnp.sin(angle)], axis=-1).reshape(NT, 2 * F) * norm
    weight = jnp.where(freqs == 0, 1.0, 2.0).astype(jnp.float32)
    inverse = jnp.stack([jnp.cos(angle).T * weight[:, None], -jnp.sin(angle).T * weight[:, None]], axis=1)
    inverse = inverse.reshape(2 * F, NT) * norm
    return (forward.astype(jnp.bfloat16), inverse.astype(jnp.bfloat16))

def per_frequency(item):
    eta = 1.0 / math.sqrt(S)
    full = item.astype(jnp.float32)
    recorded = ((full + jnp.swapaxes(full, 1, 2)) * 0.5).astype(jnp.bfloat16)
    real_part = recorded[0].astype(jnp.float32)
    imag_part = recorded[1].astype(jnp.float32)

    def mult(a, b):
        return jnp.dot(a, b, precision=lax.Precision.HIGHEST)
    square_re = mult(real_part, real_part) - mult(imag_part, imag_part)
    square_im = mult(real_part, imag_part) + mult(imag_part, real_part)
    sum_re = (real_part + eta * square_re).astype(jnp.bfloat16)
    sum_im = (imag_part + eta * square_im).astype(jnp.bfloat16)
    sum_re = lax.optimization_barrier(sum_re).astype(jnp.float32)
    sum_im = lax.optimization_barrier(sum_im).astype(jnp.float32)
    pred_re = eta * (mult(real_part, sum_re) - mult(imag_part, sum_im))
    pred_im = eta * (mult(real_part, sum_im) + mult(imag_part, sum_re))
    return jnp.stack([pred_re, pred_im]).astype(jnp.bfloat16)

def reference(traces):
    forward, inverse = make_tables()
    spectrum = jnp.einsum('srt,tk->ksr', traces.astype(jnp.float32), forward.astype(jnp.float32), precision=lax.Precision.HIGHEST)
    spectrum = spectrum.astype(jnp.bfloat16).reshape(F, 2, S, S)
    predicted = lax.map(per_frequency, spectrum)
    flat = predicted.reshape(2 * F, S, S).astype(jnp.float32)
    multiples = jnp.einsum('ksr,kt->srt', flat, inverse.astype(jnp.float32), precision=lax.Precision.HIGHEST)
    return multiples.astype(jnp.bfloat16)
```

```python
import math

import jax
import jax.numpy as jnp
import numpy as np
from jax import lax
from jax.sharding import PartitionSpec as P

F = 128
CHUNKS = 4


def make_tables(nt):
    times = np.arange(nt, dtype=np.int64)
    freqs = np.arange(F, dtype=np.int64)
    angle = ((times[:, None] * freqs[None, :]) % nt).astype(np.float32) * np.float32(2.0 * math.pi / nt)
    norm = np.float32(1.0 / math.sqrt(nt))
    forward = np.stack([np.cos(angle), -np.sin(angle)], axis=-1) * norm
    weight = np.where(freqs == 0, 1.0, 2.0).astype(np.float32)
    inverse = np.stack([np.cos(angle).T * weight[:, None], -np.sin(angle).T * weight[:, None]], axis=1) * norm
    return forward.astype(jnp.bfloat16), inverse.astype(jnp.bfloat16)


def average_pairs(first, second):
    return ((first.astype(jnp.float32) + second.astype(jnp.float32)) * 0.5).astype(jnp.bfloat16)


def batched(left, right):
    return jnp.einsum("kij,kjl->kil", left, right, preferred_element_type=jnp.float32)


def predict(recorded):
    eta = 1.0 / math.sqrt(recorded.shape[-1])
    real_part = recorded[:, 0]
    imag_part = recorded[:, 1]
    square_re = batched(real_part, real_part) - batched(imag_part, imag_part)
    square_im = batched(real_part, imag_part) + batched(imag_part, real_part)
    sum_re = (real_part.astype(jnp.float32) + eta * square_re).astype(jnp.bfloat16)
    sum_im = (imag_part.astype(jnp.float32) + eta * square_im).astype(jnp.bfloat16)
    pred_re = eta * (batched(real_part, sum_re) - batched(imag_part, sum_im))
    pred_im = eta * (batched(real_part, sum_im) + batched(imag_part, sum_re))
    return jnp.stack([pred_re, pred_im], axis=1).astype(jnp.bfloat16)


def local(traces):
    count = lax.axis_size("tile")
    rows, size, nt = traces.shape
    per_owner = F // count
    chunks = math.gcd(CHUNKS, per_owner)
    width = per_owner // chunks
    forward, inverse = make_tables(nt)
    forward = forward.reshape(nt, count, chunks, width, 2)
    inverse = inverse.reshape(count, chunks, width, 2, nt)
    parts = []
    for chunk in range(chunks):
        table = jnp.asarray(np.ascontiguousarray(forward[:, :, chunk]).reshape(nt, -1))
        spectrum = jnp.einsum("srt,tk->ksr", traces, table, preferred_element_type=jnp.float32)
        grouped = spectrum.astype(jnp.bfloat16).reshape(count, width, 2, rows, size)
        whole = lax.all_to_all(grouped, "tile", split_axis=0, concat_axis=3, tiled=True)[0]
        whole = average_pairs(whole, jnp.swapaxes(whole, 2, 3))
        predicted = predict(whole)
        shaped = predicted.reshape(1, width, 2, count, rows, size)
        returned = lax.all_to_all(shaped, "tile", split_axis=3, concat_axis=0, tiled=True)
        parts.append(returned.reshape(count * width * 2, rows, size))
    order = np.stack([inverse[:, chunk] for chunk in range(chunks)]).reshape(-1, nt)
    result = jnp.concatenate(parts, axis=0)
    multiples = jnp.einsum("kab,kt->abt", result, jnp.asarray(order), preferred_element_type=jnp.float32)
    return multiples.astype(jnp.bfloat16)


def solution(mesh):
    return jax.shard_map(
        local,
        mesh=mesh,
        in_specs=(P(("lines", "tile"), None, None),),
        out_specs=P(("lines", "tile"), None, None),
        check_vma=False,
    )
```

```python
import functools
import math

import jax
import jax.numpy as jnp
import numpy as np
from jax import lax
from jax.experimental import pallas as pl
from jax.experimental.pallas import tpu as pltpu
from jax.sharding import Mesh
from jax.sharding import PartitionSpec as P

F = 128
TILE_AXES = ("half", "side", "column")


def make_tables(nt):
    times = np.arange(nt, dtype=np.int64)
    freqs = np.arange(F, dtype=np.int64)
    angle = ((times[:, None] * freqs[None, :]) % nt).astype(np.float32) * np.float32(2.0 * math.pi / nt)
    norm = np.float32(1.0 / math.sqrt(nt))
    forward = np.stack([np.cos(angle), -np.sin(angle)], axis=-1) * norm
    weight = np.where(freqs == 0, 1.0, 2.0).astype(np.float32)
    inverse = np.stack([np.cos(angle).T * weight[:, None], -np.sin(angle).T * weight[:, None]], axis=1) * norm
    return forward.astype(jnp.bfloat16), inverse.astype(jnp.bfloat16)


def split(total):
    short = max(1, total // 16)
    long = max(1, total // 8)
    sizes = [short]
    while sum(sizes) + long + short <= total:
        sizes.append(long)
    rest = total - sum(sizes)
    if rest:
        sizes.append(rest)
    return sizes


def grid_masks(size):
    row = lax.broadcasted_iota(jnp.int32, (size, size), 0)
    col = lax.broadcasted_iota(jnp.int32, (size, size), 1)
    return row, col


def pack_kernel(half_ref, mine_ref, other_ref, own_ref, cross_ref, late_ref, a_ref):
    width, rows = mine_ref.shape[0], mine_ref.shape[3]
    slab = width * rows
    size = 2 * slab
    half = half_ref[0]
    inner = pl.multiple_of((1 - half) * slab, slab)
    outer = pl.multiple_of(half * slab, slab)
    near = pl.multiple_of(half * size, size)
    far = pl.multiple_of((1 - half) * size, size)
    for c in range(2):
        a_ref[c, pl.ds(inner, slab), :] = mine_ref[:, 0, c].reshape(slab, 2 * size)
        a_ref[c, pl.ds(outer, slab), :] = other_ref[:, 0, c].reshape(slab, 2 * size)
    own = []
    for c in range(2):
        block = a_ref[c, :, pl.ds(near, size)].astype(jnp.float32)
        own.append(((block + block.T) * 0.5).astype(jnp.bfloat16))
        own_ref[0, c] = own[c]
        cross_ref[0, c] = a_ref[c, :, pl.ds(far, size)]
        late_ref[0, c * slab : (c + 1) * slab] = a_ref[c, pl.ds(outer, slab), pl.ds(far, size)]
    row, col = grid_masks(size)
    real, imag = own[0].astype(jnp.float32), own[1].astype(jnp.float32)
    late_ref[0, 2 * slab : 2 * slab + size] = jnp.where(row <= col, real, imag).astype(jnp.bfloat16)
    diagonal = jnp.sum(jnp.where(row == col, imag, 0.0), axis=0, keepdims=True)
    tail = late_ref.shape[1] - 2 * slab - size
    late_ref[0, 2 * slab + size :] = jnp.broadcast_to(diagonal, (tail, size)).astype(jnp.bfloat16)


def product_kernel(half_ref, own_ref, cross_ref, early_ref, late_ref, inner_ref, outer_ref, y_ref, lhs_ref, rhs_ref, sum_ref):
    width, rows = early_ref.shape[0], early_ref.shape[3]
    slab = width * rows
    size = 2 * slab
    full = 2 * size
    eta = 1.0 / math.sqrt(full)
    half = half_ref[0]
    inner = pl.multiple_of((1 - half) * slab, slab)
    outer = pl.multiple_of(half * slab, slab)
    near = pl.multiple_of(half * size, size)
    far = pl.multiple_of((1 - half) * size, size)
    row, col = grid_masks(size)
    packed = late_ref[0, 2 * slab : 2 * slab + size].astype(jnp.float32)
    turned = packed.T
    diagonal = late_ref[0, 2 * slab + size :].astype(jnp.float32)[0:1]
    there = (
        jnp.where(row <= col, packed, turned),
        jnp.where(row > col, packed, jnp.where(row < col, turned, diagonal)),
    )
    for c in range(2):
        y_ref[c, pl.ds(outer, slab), :] = early_ref[:, 0, c].reshape(slab, size)
        y_ref[c, pl.ds(inner, slab), :] = late_ref[0, c * slab : (c + 1) * slab]
    for c in range(2):
        mixed = (cross_ref[0, c].astype(jnp.float32) + y_ref[c].astype(jnp.float32).T) * 0.5
        mixed = mixed.astype(jnp.bfloat16)
        turned = mixed.astype(jnp.float32).T.astype(jnp.bfloat16)
        base = c * full
        rhs_ref[base : base + size, 0:size] = own_ref[0, c]
        rhs_ref[base : base + size, size:full] = mixed
        rhs_ref[base + size : base + full, 0:size] = turned
        rhs_ref[base + size : base + full, size:full] = there[c].astype(jnp.bfloat16)
    lhs_ref[0:full, 0:full] = rhs_ref[0:full]
    lhs_ref[full:, full:] = rhs_ref[0:full]
    lhs_ref[full:, 0:full] = rhs_ref[full:]
    lhs_ref[0:full, full:] = -rhs_ref[full:]

    @pl.loop(0, 4)
    def _(step):
        at = pl.ds(pl.multiple_of(step * size, size), size)
        square = jnp.dot(lhs_ref[at, :], rhs_ref[...], preferred_element_type=jnp.float32)
        sum_ref[at, :] = (rhs_ref[at, :].astype(jnp.float32) + eta * square).astype(jnp.bfloat16)

    for c in range(2):
        for start, out_ref in ((inner, inner_ref), (outer, outer_ref)):
            left = lhs_ref[pl.ds(pl.multiple_of(c * full + start, slab), slab), :]
            value = eta * jnp.dot(left, sum_ref[...], preferred_element_type=jnp.float32)
            value = value.astype(jnp.bfloat16).reshape(width, rows, full)
            out_ref[:, 0, c, :, pl.ds(near, size)] = value[:, :, 0:size]
            out_ref[:, 0, c, :, pl.ds(far, size)] = value[:, :, size:full]


def pack(half, mine, other):
    width, count, _, rows, full = mine.shape
    slab = width * rows
    size = 2 * slab
    late = 2 * slab + size + 16
    slabs = pl.BlockSpec((width, 1, 2, rows, full), lambda k, h: (0, k, 0, 0, 0))
    square = pl.BlockSpec((1, 2, size, size), lambda k, h: (k, 0, 0, 0))
    return pl.pallas_call(
        pack_kernel,
        out_shape=(
            jax.ShapeDtypeStruct((count, 2, size, size), jnp.bfloat16),
            jax.ShapeDtypeStruct((count, 2, size, size), jnp.bfloat16),
            jax.ShapeDtypeStruct((count, late, size), jnp.bfloat16),
        ),
        grid_spec=pltpu.PrefetchScalarGridSpec(
            num_scalar_prefetch=1,
            grid=(count,),
            in_specs=[slabs, slabs],
            out_specs=[square, square, pl.BlockSpec((1, late, size), lambda k, h: (k, 0, 0))],
            scratch_shapes=[pltpu.VMEM((2, size, full), jnp.bfloat16)],
        ),
        compiler_params=pltpu.CompilerParams(vmem_limit_bytes=24 << 20),
        cost_estimate=pl.CostEstimate(flops=count * size * size * 8, bytes_accessed=count * full * full * 8, transcendentals=0),
        name="pack",
    )(half, mine, other)


def products(half, own, cross, early, late):
    width, count, _, rows, size = early.shape
    full = 2 * size
    square = pl.BlockSpec((1, 2, size, size), lambda k, h: (k, 0, 0, 0))
    slabs = pl.BlockSpec((width, 1, 2, rows, full), lambda k, h: (0, k, 0, 0, 0))
    shape = jax.ShapeDtypeStruct((width, count, 2, rows, full), jnp.bfloat16)
    return pl.pallas_call(
        product_kernel,
        out_shape=(shape, shape),
        grid_spec=pltpu.PrefetchScalarGridSpec(
            num_scalar_prefetch=1,
            grid=(count,),
            in_specs=[
                square,
                square,
                pl.BlockSpec((width, 1, 2, rows, size), lambda k, h: (0, k, 0, 0, 0)),
                pl.BlockSpec((1,) + late.shape[1:], lambda k, h: (k, 0, 0)),
            ],
            out_specs=[slabs, slabs],
            scratch_shapes=[
                pltpu.VMEM((2, size, size), jnp.bfloat16),
                pltpu.VMEM((2 * full, 2 * full), jnp.bfloat16),
                pltpu.VMEM((2 * full, full), jnp.bfloat16),
                pltpu.VMEM((2 * full, full), jnp.bfloat16),
            ],
        ),
        compiler_params=pltpu.CompilerParams(vmem_limit_bytes=32 << 20),
        cost_estimate=pl.CostEstimate(flops=count * full**3 * 12, bytes_accessed=count * full * full * 8, transcendentals=0),
        name="products",
    )(half, own, cross, early, late)


def local(width, traces):
    rows, size, nt = traces.shape
    half = lax.axis_index("half")
    flag = half.astype(jnp.int32).reshape(1)
    is_inner = lax.axis_index("side") != half

    def place(side, column):
        return side * width + column

    def permute(value, pairs):
        perm = [(place(a, k), place(b, k)) for a, b in pairs for k in range(width)]
        return lax.ppermute(value, TILE_AXES, perm)

    inward = ((0, 1), (3, 2))
    across = ((1, 2), (2, 1))
    outward = ((1, 0), (2, 3))

    per_column = F // width
    sizes = split(per_column)
    forward, inverse = make_tables(nt)
    forward = forward.reshape(nt, width, per_column, 2)
    inverse = inverse.reshape(width, per_column, 2, nt)
    starts = np.cumsum([0] + sizes)
    columns = [forward[:, :, a : a + n].reshape(nt, -1) for a, n in zip(starts, sizes)]

    def transform(table):
        table = jnp.asarray(np.ascontiguousarray(table))
        spectrum = jnp.einsum("srt,tk->ksr", traces, table, preferred_element_type=jnp.float32)
        return spectrum.astype(jnp.bfloat16)

    first = transform(columns[0])
    rest = transform(np.concatenate(columns[1:], axis=1))
    parts, at = [], 0
    for index, n in enumerate(sizes):
        if index == 0:
            spectrum = first
        else:
            spectrum = rest[at : at + width * n * 2]
            at += width * n * 2
        spectrum = spectrum.reshape(width, n, 2, rows, size)
        mine = lax.all_to_all(spectrum, "column", split_axis=0, concat_axis=0, tiled=True)
        other = permute(mine, inward)
        early = lax.dynamic_slice_in_dim(mine, (1 - half) * (size // 2), size // 2, axis=4)
        early = permute(early, across)
        own, cross, late = pack(flag, mine, other)
        late = permute(late, across)
        inner, outer = products(flag, own, cross, early, late)
        passed = permute(outer, outward)
        predicted = jnp.where(is_inner, inner, passed)
        returned = lax.all_to_all(predicted, "column", split_axis=0, concat_axis=0, tiled=True)
        parts.append(returned.reshape(width * n * 2, rows, size))
    order = np.concatenate([inverse[:, a : a + n].reshape(-1, nt) for a, n in zip(starts, sizes)])
    result = jnp.concatenate(parts, axis=0)
    multiples = jnp.einsum("kab,kt->abt", result, jnp.asarray(order), preferred_element_type=jnp.float32)
    return multiples.astype(jnp.bfloat16)


def solution(mesh):
    lines, count = mesh.shape["lines"], mesh.shape["tile"]
    width = count // 4
    inside = Mesh(mesh.devices.reshape(lines, 2, 2, width), ("lines",) + TILE_AXES)
    spec = P(("lines",) + TILE_AXES, None, None)
    return jax.shard_map(functools.partial(local, width), mesh=inside, in_specs=(spec,), out_specs=spec, check_vma=False)
```

```python
import math

import jax
import jax.numpy as jnp
import numpy as np
from jax import lax
from jax.experimental import pallas as pl
from jax.experimental.pallas import tpu as pltpu
from jax.sharding import Mesh
from jax.sharding import PartitionSpec as P

F = 128
VMEM = 60 << 20


def make_tables(nt):
    times = np.arange(nt, dtype=np.int64)
    freqs = np.arange(F, dtype=np.int64)
    angle = ((times[:, None] * freqs[None, :]) % nt).astype(np.float32) * np.float32(2.0 * math.pi / nt)
    norm = np.float32(1.0 / math.sqrt(nt))
    forward = np.stack([np.cos(angle), -np.sin(angle)], axis=-1) * norm
    weight = np.where(freqs == 0, 1.0, 2.0).astype(np.float32)
    inverse = np.stack([np.cos(angle).T * weight[:, None], -np.sin(angle).T * weight[:, None]], axis=1) * norm
    return forward.astype(jnp.bfloat16), inverse.astype(jnp.bfloat16)


def split(group):
    share = F // group
    chunks = math.gcd(4, share)
    return [share // chunks] * chunks


def grid_masks(size):
    row = lax.broadcasted_iota(jnp.int32, (size, size), 0)
    col = lax.broadcasted_iota(jnp.int32, (size, size), 1)
    return row, col


def forward_kernel(traces_ref, table_ref, *refs):
    outs, scratch = refs[:-1], refs[-1]
    rows = traces_ref.shape[0]
    count = table_ref.shape[0]
    for s in range(rows):
        value = lax.dot_general(
            table_ref[...], traces_ref[s], (((1,), (1,)), ((), ())), preferred_element_type=jnp.float32
        )
        for lane in range(scratch.shape[0]):
            scratch[lane, pl.ds(s, count, stride=rows), :] = value[:, lane * 128 : (lane + 1) * 128]
    at = 0
    for out in outs:
        n = out.shape[0]
        for lane in range(scratch.shape[0]):
            piece = scratch[lane, at * rows : (at + n) * rows, :].reshape(n, rows, 128)
            out[:, :, lane * 128 : (lane + 1) * 128] = piece.astype(jnp.bfloat16)
        at += n


def inverse_kernel(*refs):
    ins, table_ref, out_ref, scratch = refs[:-3], refs[-3], refs[-2], refs[-1]
    rows = out_ref.shape[0]
    count = table_ref.shape[0]
    at = 0
    for ref in ins:
        n = ref.shape[0]
        for lane in range(scratch.shape[0]):
            piece = ref[:, :, lane * 128 : (lane + 1) * 128].astype(jnp.float32)
            scratch[lane, at * rows : (at + n) * rows, :] = piece.reshape(n * rows, 128)
        at += n
    for s in range(rows):
        for lane in range(scratch.shape[0]):
            value = scratch[lane, pl.ds(s, count, stride=rows), :]
            value = lax.dot_general(
                value.T.astype(jnp.bfloat16), table_ref[...], (((1,), (0,)), ((), ())), preferred_element_type=jnp.float32
            )
            out_ref[s, lane * 128 : (lane + 1) * 128, :] = value.astype(jnp.bfloat16)


def transform(traces, table, counts):
    rows, size, nt = traces.shape
    total = table.shape[0]
    block = min(rows, 16)
    lanes = min(size, 256)
    return pl.pallas_call(
        forward_kernel,
        out_shape=tuple(jax.ShapeDtypeStruct((n, rows, size), jnp.bfloat16) for n in counts),
        grid=(rows // block, size // lanes),
        in_specs=[
            pl.BlockSpec((block, lanes, nt), lambda i, j: (i, j, 0)),
            pl.BlockSpec((total, nt), lambda i, j: (0, 0)),
        ],
        out_specs=tuple(pl.BlockSpec((n, block, lanes), lambda i, j: (0, i, j)) for n in counts),
        scratch_shapes=[pltpu.VMEM((lanes // 128, total * block, 128), jnp.float32)],
        compiler_params=pltpu.CompilerParams(vmem_limit_bytes=VMEM),
        cost_estimate=pl.CostEstimate(
            flops=2 * rows * size * nt * total, bytes_accessed=2 * rows * size * (nt + total), transcendentals=0
        ),
        name="transform",
    )(traces, table)


def restore(parts, table):
    rows, size = parts[0].shape[1:]
    total, nt = table.shape
    block = min(rows, 16)
    lanes = min(size, 256)
    return pl.pallas_call(
        inverse_kernel,
        out_shape=jax.ShapeDtypeStruct((rows, size, nt), jnp.bfloat16),
        grid=(rows // block, size // lanes),
        in_specs=[pl.BlockSpec((p.shape[0], block, lanes), lambda i, j: (0, i, j)) for p in parts]
        + [pl.BlockSpec((total, nt), lambda i, j: (0, 0))],
        out_specs=pl.BlockSpec((block, lanes, nt), lambda i, j: (i, j, 0)),
        scratch_shapes=[pltpu.VMEM((lanes // 128, total * block, 128), jnp.float32)],
        compiler_params=pltpu.CompilerParams(vmem_limit_bytes=VMEM),
        cost_estimate=pl.CostEstimate(
            flops=2 * rows * size * nt * total, bytes_accessed=2 * rows * size * (nt + total), transcendentals=0
        ),
        name="restore",
    )(*parts, table)


def pack_kernel(half_ref, mine_ref, own_ref, sent_ref):
    size = own_ref.shape[2]
    half = half_ref[0]
    near = pl.multiple_of(half * size, size)
    far = pl.multiple_of((1 - half) * size, size)
    own = []
    for c in range(2):
        block = mine_ref[:, 0, c, :, pl.ds(near, size)].reshape(size, size).astype(jnp.float32)
        own.append(((block + block.T) * 0.5).astype(jnp.bfloat16))
        own_ref[0, c] = own[c]
        sent_ref[0, c * size : (c + 1) * size] = mine_ref[:, 0, c, :, pl.ds(far, size)].reshape(size, size)
    row, col = grid_masks(size)
    real, imag = own[0].astype(jnp.float32), own[1].astype(jnp.float32)
    sent_ref[0, 2 * size : 3 * size] = jnp.where(row <= col, real, imag).astype(jnp.bfloat16)
    diagonal = jnp.sum(jnp.where(row == col, imag, 0.0), axis=0, keepdims=True)
    tail = sent_ref.shape[1] - 3 * size
    sent_ref[0, 3 * size :] = jnp.broadcast_to(diagonal, (tail, size)).astype(jnp.bfloat16)


def product_kernel(half_ref, own_ref, sent_ref, got_ref, out_ref, lhs_ref, rhs_ref, sum_ref):
    group, rows, full = out_ref.shape[0], out_ref.shape[3], out_ref.shape[4]
    size = full // 2
    eta = 1.0 / math.sqrt(full)
    half = half_ref[0]
    near = pl.multiple_of(half * size, size)
    far = pl.multiple_of((1 - half) * size, size)
    row, col = grid_masks(size)
    packed = got_ref[0, 2 * size : 3 * size].astype(jnp.float32)
    turned = packed.T
    diagonal = got_ref[0, 3 * size :].astype(jnp.float32)[0:1]
    there = (
        jnp.where(row <= col, packed, turned),
        jnp.where(row > col, packed, jnp.where(row < col, turned, diagonal)),
    )
    for c in range(2):
        at = slice(c * size, (c + 1) * size)
        mixed = (sent_ref[0, at].astype(jnp.float32) + got_ref[0, at].astype(jnp.float32).T) * 0.5
        mixed = mixed.astype(jnp.bfloat16)
        turned = mixed.astype(jnp.float32).T.astype(jnp.bfloat16)
        base = c * full
        rhs_ref[base : base + size, 0:size] = own_ref[0, c]
        rhs_ref[base : base + size, size:full] = mixed
        rhs_ref[base + size : base + full, 0:size] = turned
        rhs_ref[base + size : base + full, size:full] = there[c].astype(jnp.bfloat16)
    lhs_ref[0:full, 0:full] = rhs_ref[0:full]
    lhs_ref[full:, full:] = rhs_ref[0:full]
    lhs_ref[full:, 0:full] = rhs_ref[full:]
    lhs_ref[0:full, full:] = -rhs_ref[full:]

    @pl.loop(0, 4)
    def _(step):
        at = pl.ds(pl.multiple_of(step * size, size), size)
        square = jnp.dot(lhs_ref[at, :], rhs_ref[...], preferred_element_type=jnp.float32)
        sum_ref[at, :] = (rhs_ref[at, :].astype(jnp.float32) + eta * square).astype(jnp.bfloat16)

    for c in range(2):
        value = jnp.dot(lhs_ref[c * full : c * full + size], sum_ref[...], preferred_element_type=jnp.float32)
        value = (eta * value).astype(jnp.bfloat16).reshape(group, rows, full)
        out_ref[:, 0, c, :, pl.ds(near, size)] = value[:, :, 0:size]
        out_ref[:, 0, c, :, pl.ds(far, size)] = value[:, :, size:full]


def pack(half, mine):
    group, count, _, rows, full = mine.shape
    size = full // 2
    sent = 3 * size + 16
    return pl.pallas_call(
        pack_kernel,
        out_shape=(
            jax.ShapeDtypeStruct((count, 2, size, size), jnp.bfloat16),
            jax.ShapeDtypeStruct((count, sent, size), jnp.bfloat16),
        ),
        grid_spec=pltpu.PrefetchScalarGridSpec(
            num_scalar_prefetch=1,
            grid=(count,),
            in_specs=[pl.BlockSpec((group, 1, 2, rows, full), lambda k, h: (0, k, 0, 0, 0))],
            out_specs=[
                pl.BlockSpec((1, 2, size, size), lambda k, h: (k, 0, 0, 0)),
                pl.BlockSpec((1, sent, size), lambda k, h: (k, 0, 0)),
            ],
        ),
        compiler_params=pltpu.CompilerParams(vmem_limit_bytes=VMEM),
        cost_estimate=pl.CostEstimate(flops=count * size * size * 8, bytes_accessed=count * full * full * 5, transcendentals=0),
        name="pack",
    )(half, mine)


def products(half, own, sent, got, group):
    count, size = own.shape[0], own.shape[2]
    full = 2 * size
    rows = size // group
    shape = jax.ShapeDtypeStruct((group, count, 2, rows, full), jnp.bfloat16)
    passed = pl.BlockSpec((1,) + got.shape[1:], lambda k, h: (k, 0, 0))
    return pl.pallas_call(
        product_kernel,
        out_shape=shape,
        grid_spec=pltpu.PrefetchScalarGridSpec(
            num_scalar_prefetch=1,
            grid=(count,),
            in_specs=[pl.BlockSpec((1, 2, size, size), lambda k, h: (k, 0, 0, 0)), passed, passed],
            out_specs=pl.BlockSpec((group, 1, 2, rows, full), lambda k, h: (0, k, 0, 0, 0)),
            scratch_shapes=[
                pltpu.VMEM((2 * full, 2 * full), jnp.bfloat16),
                pltpu.VMEM((2 * full, full), jnp.bfloat16),
                pltpu.VMEM((2 * full, full), jnp.bfloat16),
            ],
        ),
        compiler_params=pltpu.CompilerParams(vmem_limit_bytes=VMEM),
        cost_estimate=pl.CostEstimate(flops=count * full**3 * 12, bytes_accessed=count * full * full * 5, transcendentals=0),
        name="products",
    )(half, own, sent, got)


def local(group, traces):
    rows, size, nt = traces.shape
    flag = lax.axis_index("half").astype(jnp.int32).reshape(1)
    chunks = split(group)
    forward, inverse = make_tables(nt)
    table = forward.reshape(nt, 2 * F).T
    spectra = transform(traces, jnp.asarray(table), [2 * group * n for n in chunks])
    parts = []
    for n, spectrum in zip(chunks, spectra):
        spectrum = spectrum.reshape(group, n, 2, rows, size)
        mine = lax.all_to_all(spectrum, "member", split_axis=0, concat_axis=0, tiled=True)
        own, sent = pack(flag, mine)
        got = lax.ppermute(sent, "half", [(0, 1), (1, 0)])
        predicted = products(flag, own, sent, got, group)
        returned = lax.all_to_all(predicted, "member", split_axis=0, concat_axis=0, tiled=True)
        parts.append(returned.reshape(group * n * 2, rows, size))
    return restore(parts, jnp.asarray(inverse.reshape(2 * F, nt)))


def solution(mesh):
    lines, count = mesh.shape["lines"], mesh.shape["tile"]
    group = count // 2
    inside = Mesh(mesh.devices.reshape(lines, 2, group), ("lines", "half", "member"))
    spec = P(inside.axis_names, None, None)

    def body(traces):
        return local(group, traces)

    return jax.shard_map(body, mesh=inside, in_specs=(spec,), out_specs=spec, check_vma=False)
```

```python
import math

import jax
import jax.numpy as jnp
import numpy as np
from jax import lax
from jax.experimental import pallas as pl
from jax.experimental.pallas import tpu as pltpu
from jax.sharding import Mesh
from jax.sharding import PartitionSpec as P

F = 128
VMEM = 60 << 20
TAIL = 16
SIZES = (3, 4, 5, 4, 16)


def make_tables(nt):
    times = np.arange(nt, dtype=np.int64)
    freqs = np.arange(F, dtype=np.int64)
    angle = ((times[:, None] * freqs[None, :]) % nt).astype(np.float32) * np.float32(2.0 * math.pi / nt)
    norm = np.float32(1.0 / math.sqrt(nt))
    forward = np.stack([np.cos(angle), -np.sin(angle)], axis=-1) * norm
    weight = np.where(freqs == 0, 1.0, 2.0).astype(np.float32)
    inverse = np.stack([np.cos(angle).T * weight[:, None], -np.sin(angle).T * weight[:, None]], axis=1) * norm
    return forward.astype(jnp.bfloat16), inverse.astype(jnp.bfloat16)


def split(group):
    share = F // group
    marks = [round(share * mark / SIZES[-1]) for mark in np.cumsum((0,) + SIZES[:-1])]
    return [b - a for a, b in zip(marks, marks[1:]) if b > a]


def grid_masks(size):
    row = lax.broadcasted_iota(jnp.int32, (size, size), 0)
    col = lax.broadcasted_iota(jnp.int32, (size, size), 1)
    return row, col


def forward_kernel(traces_ref, table_ref, *refs):
    outs, scratch = refs[:-1], refs[-1]
    rows = traces_ref.shape[0]
    count = table_ref.shape[0]
    for s in range(rows):
        value = lax.dot_general(
            table_ref[...], traces_ref[s], (((1,), (1,)), ((), ())), preferred_element_type=jnp.float32
        )
        for lane in range(scratch.shape[0]):
            scratch[lane, pl.ds(s, count, stride=rows), :] = value[:, lane * 128 : (lane + 1) * 128]
    at = 0
    for out in outs:
        n = out.shape[0]
        for lane in range(scratch.shape[0]):
            piece = scratch[lane, at * rows : (at + n) * rows, :].reshape(n, rows, 128)
            out[:, :, lane * 128 : (lane + 1) * 128] = piece.astype(jnp.bfloat16)
        at += n


def inverse_kernel(*refs):
    ins, table_ref, out_ref, scratch = refs[:-3], refs[-3], refs[-2], refs[-1]
    rows = out_ref.shape[0]
    count = table_ref.shape[0]
    at = 0
    for ref in ins:
        n = ref.shape[0]
        for lane in range(scratch.shape[0]):
            piece = ref[:, :, lane * 128 : (lane + 1) * 128].astype(jnp.float32)
            scratch[lane, at * rows : (at + n) * rows, :] = piece.reshape(n * rows, 128)
        at += n
    for s in range(rows):
        lanes = [scratch[lane, pl.ds(s, count, stride=rows), :] for lane in range(scratch.shape[0])]
        value = jnp.concatenate(lanes, axis=1).T.astype(jnp.bfloat16)
        out_ref[s] = jnp.dot(value, table_ref[...], preferred_element_type=jnp.float32).astype(jnp.bfloat16)


def transform(traces, table, counts):
    rows, size, nt = traces.shape
    total = table.shape[0]
    block = min(rows, 16)
    lanes = min(size, 256)
    return pl.pallas_call(
        forward_kernel,
        out_shape=tuple(jax.ShapeDtypeStruct((n, rows, size), jnp.bfloat16) for n in counts),
        grid=(rows // block, size // lanes),
        in_specs=[
            pl.BlockSpec((block, lanes, nt), lambda i, j: (i, j, 0)),
            pl.BlockSpec((total, nt), lambda i, j: (0, 0)),
        ],
        out_specs=tuple(pl.BlockSpec((n, block, lanes), lambda i, j: (0, i, j)) for n in counts),
        scratch_shapes=[pltpu.VMEM((lanes // 128, total * block, 128), jnp.float32)],
        compiler_params=pltpu.CompilerParams(vmem_limit_bytes=VMEM),
        cost_estimate=pl.CostEstimate(
            flops=2 * rows * size * nt * total, bytes_accessed=2 * rows * size * (nt + total), transcendentals=0
        ),
        name="transform",
    )(traces, table)


def restore(parts, table):
    rows, size = parts[0].shape[1:]
    total, nt = table.shape
    block = min(rows, 16)
    lanes = min(size, 256)
    return pl.pallas_call(
        inverse_kernel,
        out_shape=jax.ShapeDtypeStruct((rows, size, nt), jnp.bfloat16),
        grid=(rows // block, size // lanes),
        in_specs=[pl.BlockSpec((p.shape[0], block, lanes), lambda i, j: (0, i, j)) for p in parts]
        + [pl.BlockSpec((total, nt), lambda i, j: (0, 0))],
        out_specs=pl.BlockSpec((block, lanes, nt), lambda i, j: (i, j, 0)),
        scratch_shapes=[pltpu.VMEM((lanes // 128, total * block, 128), jnp.float32)],
        compiler_params=pltpu.CompilerParams(vmem_limit_bytes=VMEM),
        cost_estimate=pl.CostEstimate(
            flops=2 * rows * size * nt * total, bytes_accessed=2 * rows * size * (nt + total), transcendentals=0
        ),
        name="restore",
    )(*parts, table)


def pack_kernel(half_ref, mine_ref, own_ref, sent_ref):
    size = own_ref.shape[2]
    half = half_ref[0]
    near = pl.multiple_of(half * size, size)
    far = pl.multiple_of((1 - half) * size, size)
    step = pl.program_id(0)
    base = step * (3 * size)
    own = []
    for c in range(2):
        block = mine_ref[:, 0, c, :, pl.ds(near, size)].reshape(size, size).astype(jnp.float32)
        own.append(((block + block.T) * 0.5).astype(jnp.bfloat16))
        own_ref[0, c] = own[c]
        at = pl.ds(pl.multiple_of(base + c * size, size), size)
        sent_ref[at] = mine_ref[:, 0, c, :, pl.ds(far, size)].reshape(size, size)
    row, col = grid_masks(size)
    real, imag = own[0].astype(jnp.float32), own[1].astype(jnp.float32)
    at = pl.ds(pl.multiple_of(base + 2 * size, size), size)
    sent_ref[at] = jnp.where(row <= col, real, imag).astype(jnp.bfloat16)
    diagonal = jnp.sum(jnp.where(row == col, imag, 0.0), axis=0, keepdims=True)
    tail = sent_ref.shape[0] - TAIL
    line = lax.broadcasted_iota(jnp.int32, (TAIL, size), 0)
    before = jnp.where(step == 0, 0.0, sent_ref[tail:].astype(jnp.float32))
    sent_ref[tail:] = jnp.where(line == step, diagonal, before).astype(jnp.bfloat16)


def product_kernel(half_ref, own_ref, sent_ref, got_ref, out_ref, lhs_ref, rhs_ref, sum_ref):
    group, rows, full = out_ref.shape[0], out_ref.shape[3], out_ref.shape[4]
    size = full // 2
    eta = 1.0 / math.sqrt(full)
    half = half_ref[0]
    near = pl.multiple_of(half * size, size)
    far = pl.multiple_of((1 - half) * size, size)
    row, col = grid_masks(size)
    step = pl.program_id(0)
    start = step * (3 * size)
    packed = got_ref[pl.ds(pl.multiple_of(start + 2 * size, size), size)].astype(jnp.float32)
    turned = packed.T
    tail = got_ref[got_ref.shape[0] - TAIL :].astype(jnp.float32)
    line = lax.broadcasted_iota(jnp.int32, (TAIL, size), 0)
    diagonal = jnp.sum(jnp.where(line == step, tail, 0.0), axis=0, keepdims=True)
    there = (
        jnp.where(row <= col, packed, turned),
        jnp.where(row > col, packed, jnp.where(row < col, turned, diagonal)),
    )
    for c in range(2):
        at = pl.ds(pl.multiple_of(start + c * size, size), size)
        mixed = (sent_ref[at].astype(jnp.float32) + got_ref[at].astype(jnp.float32).T) * 0.5
        mixed = mixed.astype(jnp.bfloat16)
        turned = mixed.astype(jnp.float32).T.astype(jnp.bfloat16)
        base = c * full
        rhs_ref[base : base + size, 0:size] = own_ref[0, c]
        rhs_ref[base : base + size, size:full] = mixed
        rhs_ref[base + size : base + full, 0:size] = turned
        rhs_ref[base + size : base + full, size:full] = there[c].astype(jnp.bfloat16)
    lhs_ref[0:full, 0:full] = rhs_ref[0:full]
    lhs_ref[full:, full:] = rhs_ref[0:full]
    lhs_ref[full:, 0:full] = rhs_ref[full:]
    lhs_ref[0:full, full:] = -rhs_ref[full:]

    @pl.loop(0, 4)
    def _(part):
        at = pl.ds(pl.multiple_of(part * size, size), size)
        square = jnp.dot(lhs_ref[at, :], rhs_ref[...], preferred_element_type=jnp.float32)
        sum_ref[at, :] = (rhs_ref[at, :].astype(jnp.float32) + eta * square).astype(jnp.bfloat16)

    for c in range(2):
        value = jnp.dot(lhs_ref[c * full : c * full + size], sum_ref[...], preferred_element_type=jnp.float32)
        value = (eta * value).astype(jnp.bfloat16).reshape(group, rows, full)
        out_ref[:, 0, c, :, pl.ds(near, size)] = value[:, :, 0:size]
        out_ref[:, 0, c, :, pl.ds(far, size)] = value[:, :, size:full]


def pack(half, mine):
    group, count, _, rows, full = mine.shape
    size = full // 2
    sent = count * 3 * size + TAIL
    return pl.pallas_call(
        pack_kernel,
        out_shape=(
            jax.ShapeDtypeStruct((count, 2, size, size), jnp.bfloat16),
            jax.ShapeDtypeStruct((sent, size), jnp.bfloat16),
        ),
        grid_spec=pltpu.PrefetchScalarGridSpec(
            num_scalar_prefetch=1,
            grid=(count,),
            in_specs=[pl.BlockSpec((group, 1, 2, rows, full), lambda k, h: (0, k, 0, 0, 0))],
            out_specs=[
                pl.BlockSpec((1, 2, size, size), lambda k, h: (k, 0, 0, 0)),
                pl.BlockSpec((sent, size), lambda k, h: (0, 0)),
            ],
        ),
        compiler_params=pltpu.CompilerParams(vmem_limit_bytes=VMEM),
        cost_estimate=pl.CostEstimate(flops=count * size * size * 8, bytes_accessed=count * full * full * 5, transcendentals=0),
        name="pack",
    )(half, mine)


def products(half, own, sent, got, group):
    count, size = own.shape[0], own.shape[2]
    full = 2 * size
    rows = size // group
    shape = jax.ShapeDtypeStruct((group, count, 2, rows, full), jnp.bfloat16)
    passed = pl.BlockSpec(got.shape, lambda k, h: (0, 0))
    return pl.pallas_call(
        product_kernel,
        out_shape=shape,
        grid_spec=pltpu.PrefetchScalarGridSpec(
            num_scalar_prefetch=1,
            grid=(count,),
            in_specs=[pl.BlockSpec((1, 2, size, size), lambda k, h: (k, 0, 0, 0)), passed, passed],
            out_specs=pl.BlockSpec((group, 1, 2, rows, full), lambda k, h: (0, k, 0, 0, 0)),
            scratch_shapes=[
                pltpu.VMEM((2 * full, 2 * full), jnp.bfloat16),
                pltpu.VMEM((2 * full, full), jnp.bfloat16),
                pltpu.VMEM((2 * full, full), jnp.bfloat16),
            ],
        ),
        compiler_params=pltpu.CompilerParams(vmem_limit_bytes=VMEM),
        cost_estimate=pl.CostEstimate(flops=count * full**3 * 12, bytes_accessed=count * full * full * 5, transcendentals=0),
        name="products",
    )(half, own, sent, got)


def local(group, traces):
    rows, size, nt = traces.shape
    flag = lax.axis_index("half").astype(jnp.int32).reshape(1)
    chunks = split(group)
    forward, inverse = make_tables(nt)
    table = forward.reshape(nt, 2 * F).T
    counts = [2 * group * n for n in chunks]
    spectra = transform(traces, jnp.asarray(table[: counts[0]]), counts[:1])
    spectra += transform(traces, jnp.asarray(table[counts[0] :]), counts[1:])
    parts = []
    for n, spectrum in zip(chunks, spectra):
        spectrum = spectrum.reshape(group, n, 2, rows, size)
        mine = lax.all_to_all(spectrum, "member", split_axis=0, concat_axis=0, tiled=True)
        own, sent = pack(flag, mine)
        got = lax.ppermute(sent, "half", [(0, 1), (1, 0)])
        predicted = products(flag, own, sent, got, group)
        returned = lax.all_to_all(predicted, "member", split_axis=0, concat_axis=0, tiled=True)
        parts.append(returned.reshape(group * n * 2, rows, size))
    return restore(parts, jnp.asarray(inverse.reshape(2 * F, nt)))


def solution(mesh):
    lines, count = mesh.shape["lines"], mesh.shape["tile"]
    group = count // 2
    inside = Mesh(mesh.devices.reshape(lines, 2, group), ("lines", "half", "member"))
    spec = P(inside.axis_names, None, None)

    def body(traces):
        return local(group, traces)

    return jax.shard_map(body, mesh=inside, in_specs=(spec,), out_specs=spec, check_vma=False)
```

```python
import math

import jax
import jax.numpy as jnp
import numpy as np
from jax import lax
from jax.experimental import pallas as pl
from jax.experimental.pallas import tpu as pltpu
from jax.sharding import Mesh
from jax.sharding import PartitionSpec as P

F = 128
VMEM = 60 << 20
TAIL = 16
SIZES = (3, 4, 5, 4, 16)


def make_tables(nt):
    times = np.arange(nt, dtype=np.int64)
    freqs = np.arange(F, dtype=np.int64)
    angle = ((times[:, None] * freqs[None, :]) % nt).astype(np.float32) * np.float32(2.0 * math.pi / nt)
    norm = np.float32(1.0 / math.sqrt(nt))
    forward = np.stack([np.cos(angle), -np.sin(angle)], axis=-1) * norm
    weight = np.where(freqs == 0, 1.0, 2.0).astype(np.float32)
    inverse = np.stack([np.cos(angle).T * weight[:, None], -np.sin(angle).T * weight[:, None]], axis=1) * norm
    return forward.astype(jnp.bfloat16), inverse.astype(jnp.bfloat16)


def split(group):
    share = F // group
    marks = [round(share * mark / SIZES[-1]) for mark in np.cumsum((0,) + SIZES[:-1])]
    return [b - a for a, b in zip(marks, marks[1:]) if b > a]


def grid_masks(size):
    row = lax.broadcasted_iota(jnp.int32, (size, size), 0)
    col = lax.broadcasted_iota(jnp.int32, (size, size), 1)
    return row, col


def forward_kernel(traces_ref, table_ref, *refs):
    outs, scratch = refs[:-1], refs[-1]
    rows = traces_ref.shape[0]
    count = table_ref.shape[0]
    for s in range(rows):
        value = lax.dot_general(
            table_ref[...], traces_ref[s], (((1,), (1,)), ((), ())), preferred_element_type=jnp.float32
        )
        for lane in range(scratch.shape[0]):
            scratch[lane, pl.ds(s, count, stride=rows), :] = value[:, lane * 128 : (lane + 1) * 128]
    at = 0
    for out in outs:
        n = out.shape[0]
        for lane in range(scratch.shape[0]):
            piece = scratch[lane, at * rows : (at + n) * rows, :].reshape(n, rows, 128)
            out[:, :, lane * 128 : (lane + 1) * 128] = piece.astype(jnp.bfloat16)
        at += n


def inverse_kernel(*refs):
    ins, table_ref, out_ref, scratch = refs[:-3], refs[-3], refs[-2], refs[-1]
    rows = out_ref.shape[0]
    count = table_ref.shape[0]
    at = 0
    for ref in ins:
        n = ref.shape[0]
        for lane in range(scratch.shape[0]):
            piece = ref[:, :, lane * 128 : (lane + 1) * 128].astype(jnp.float32)
            scratch[lane, at * rows : (at + n) * rows, :] = piece.reshape(n * rows, 128)
        at += n
    for s in range(rows):
        lanes = [scratch[lane, pl.ds(s, count, stride=rows), :] for lane in range(scratch.shape[0])]
        value = jnp.concatenate(lanes, axis=1).T.astype(jnp.bfloat16)
        out_ref[s] = jnp.dot(value, table_ref[...], preferred_element_type=jnp.float32).astype(jnp.bfloat16)


def transform(traces, table, counts):
    rows, size, nt = traces.shape
    total = table.shape[0]
    block = min(rows, 16)
    lanes = min(size, 256)
    return pl.pallas_call(
        forward_kernel,
        out_shape=tuple(jax.ShapeDtypeStruct((n, rows, size), jnp.bfloat16) for n in counts),
        grid=(rows // block, size // lanes),
        in_specs=[
            pl.BlockSpec((block, lanes, nt), lambda i, j: (i, j, 0)),
            pl.BlockSpec((total, nt), lambda i, j: (0, 0)),
        ],
        out_specs=tuple(pl.BlockSpec((n, block, lanes), lambda i, j: (0, i, j)) for n in counts),
        scratch_shapes=[pltpu.VMEM((lanes // 128, total * block, 128), jnp.float32)],
        compiler_params=pltpu.CompilerParams(vmem_limit_bytes=VMEM),
        cost_estimate=pl.CostEstimate(
            flops=2 * rows * size * nt * total, bytes_accessed=2 * rows * size * (nt + total), transcendentals=0
        ),
        name="transform",
    )(traces, table)


def restore(parts, table):
    rows, size = parts[0].shape[1:]
    total, nt = table.shape
    block = min(rows, 16)
    lanes = min(size, 256)
    return pl.pallas_call(
        inverse_kernel,
        out_shape=jax.ShapeDtypeStruct((rows, size, nt), jnp.bfloat16),
        grid=(rows // block, size // lanes),
        in_specs=[pl.BlockSpec((p.shape[0], block, lanes), lambda i, j: (0, i, j)) for p in parts]
        + [pl.BlockSpec((total, nt), lambda i, j: (0, 0))],
        out_specs=pl.BlockSpec((block, lanes, nt), lambda i, j: (i, j, 0)),
        scratch_shapes=[pltpu.VMEM((lanes // 128, total * block, 128), jnp.float32)],
        compiler_params=pltpu.CompilerParams(vmem_limit_bytes=VMEM),
        cost_estimate=pl.CostEstimate(
            flops=2 * rows * size * nt * total, bytes_accessed=2 * rows * size * (nt + total), transcendentals=0
        ),
        name="restore",
    )(*parts, table)


def pack_kernel(half_ref, mine_ref, own_ref, sent_ref):
    size = own_ref.shape[2]
    half = half_ref[0]
    near = pl.multiple_of(half * size, size)
    far = pl.multiple_of((1 - half) * size, size)
    step = pl.program_id(0)
    base = step * (3 * size)
    own = []
    for c in range(2):
        block = mine_ref[:, 0, c, :, pl.ds(near, size)].reshape(size, size).astype(jnp.float32)
        own.append(((block + block.T) * 0.5).astype(jnp.bfloat16))
        own_ref[0, c] = own[c]
        at = pl.ds(pl.multiple_of(base + c * size, size), size)
        sent_ref[at] = mine_ref[:, 0, c, :, pl.ds(far, size)].reshape(size, size)
    row, col = grid_masks(size)
    real, imag = own[0].astype(jnp.float32), own[1].astype(jnp.float32)
    at = pl.ds(pl.multiple_of(base + 2 * size, size), size)
    sent_ref[at] = jnp.where(row <= col, real, imag).astype(jnp.bfloat16)
    diagonal = jnp.sum(jnp.where(row == col, imag, 0.0), axis=0, keepdims=True)
    tail = sent_ref.shape[0] - TAIL
    line = lax.broadcasted_iota(jnp.int32, (TAIL, size), 0)
    before = jnp.where(step == 0, 0.0, sent_ref[tail:].astype(jnp.float32))
    sent_ref[tail:] = jnp.where(line == step, diagonal, before).astype(jnp.bfloat16)


def product_kernel(half_ref, own_ref, sent_ref, got_ref, tail_ref, out_ref, lhs_ref, rhs_ref, sum_ref):
    group, rows, full = out_ref.shape[0], out_ref.shape[3], out_ref.shape[4]
    size = full // 2
    eta = 1.0 / math.sqrt(full)
    half = half_ref[0]
    near = pl.multiple_of(half * size, size)
    far = pl.multiple_of((1 - half) * size, size)
    row, col = grid_masks(size)
    step = pl.program_id(0)
    packed = got_ref[2 * size : 3 * size].astype(jnp.float32)
    turned = packed.T
    tail = tail_ref[...].astype(jnp.float32)
    line = lax.broadcasted_iota(jnp.int32, (TAIL, size), 0)
    diagonal = jnp.sum(jnp.where(line == step, tail, 0.0), axis=0, keepdims=True)
    there = (
        jnp.where(row <= col, packed, turned),
        jnp.where(row > col, packed, jnp.where(row < col, turned, diagonal)),
    )
    for c in range(2):
        at = slice(c * size, (c + 1) * size)
        mixed = (sent_ref[at].astype(jnp.float32) + got_ref[at].astype(jnp.float32).T) * 0.5
        mixed = mixed.astype(jnp.bfloat16)
        turned = mixed.astype(jnp.float32).T.astype(jnp.bfloat16)
        base = c * full
        rhs_ref[base : base + size, 0:size] = own_ref[0, c]
        rhs_ref[base : base + size, size:full] = mixed
        rhs_ref[base + size : base + full, 0:size] = turned
        rhs_ref[base + size : base + full, size:full] = there[c].astype(jnp.bfloat16)
    lhs_ref[0:full, 0:full] = rhs_ref[0:full]
    lhs_ref[full:, full:] = rhs_ref[0:full]
    lhs_ref[full:, 0:full] = rhs_ref[full:]
    lhs_ref[0:full, full:] = -rhs_ref[full:]

    @pl.loop(0, 4)
    def _(part):
        at = pl.ds(pl.multiple_of(part * size, size), size)
        square = jnp.dot(lhs_ref[at, :], rhs_ref[...], preferred_element_type=jnp.float32)
        sum_ref[at, :] = (rhs_ref[at, :].astype(jnp.float32) + eta * square).astype(jnp.bfloat16)

    for c in range(2):
        value = jnp.dot(lhs_ref[c * full : c * full + size], sum_ref[...], preferred_element_type=jnp.float32)
        value = (eta * value).astype(jnp.bfloat16).reshape(group, rows, full)
        out_ref[:, 0, c, :, pl.ds(near, size)] = value[:, :, 0:size]
        out_ref[:, 0, c, :, pl.ds(far, size)] = value[:, :, size:full]


def pack(half, mine):
    group, count, _, rows, full = mine.shape
    size = full // 2
    sent = count * 3 * size + TAIL
    return pl.pallas_call(
        pack_kernel,
        out_shape=(
            jax.ShapeDtypeStruct((count, 2, size, size), jnp.bfloat16),
            jax.ShapeDtypeStruct((sent, size), jnp.bfloat16),
        ),
        grid_spec=pltpu.PrefetchScalarGridSpec(
            num_scalar_prefetch=1,
            grid=(count,),
            in_specs=[pl.BlockSpec((group, 1, 2, rows, full), lambda k, h: (0, k, 0, 0, 0))],
            out_specs=[
                pl.BlockSpec((1, 2, size, size), lambda k, h: (k, 0, 0, 0)),
                pl.BlockSpec((sent, size), lambda k, h: (0, 0)),
            ],
        ),
        compiler_params=pltpu.CompilerParams(vmem_limit_bytes=VMEM),
        cost_estimate=pl.CostEstimate(flops=count * size * size * 8, bytes_accessed=count * full * full * 5, transcendentals=0),
        name="pack",
    )(half, mine)


def products(half, own, sent, got, group):
    count, size = own.shape[0], own.shape[2]
    full = 2 * size
    rows = size // group
    shape = jax.ShapeDtypeStruct((group, count, 2, rows, full), jnp.bfloat16)
    passed = pl.BlockSpec((3 * size, size), lambda k, h: (k, 0))
    last = pl.BlockSpec((TAIL, size), lambda k, h: (count * 3 * size // TAIL, 0))
    return pl.pallas_call(
        product_kernel,
        out_shape=shape,
        grid_spec=pltpu.PrefetchScalarGridSpec(
            num_scalar_prefetch=1,
            grid=(count,),
            in_specs=[pl.BlockSpec((1, 2, size, size), lambda k, h: (k, 0, 0, 0)), passed, passed, last],
            out_specs=pl.BlockSpec((group, 1, 2, rows, full), lambda k, h: (0, k, 0, 0, 0)),
            scratch_shapes=[
                pltpu.VMEM((2 * full, 2 * full), jnp.bfloat16),
                pltpu.VMEM((2 * full, full), jnp.bfloat16),
                pltpu.VMEM((2 * full, full), jnp.bfloat16),
            ],
        ),
        compiler_params=pltpu.CompilerParams(vmem_limit_bytes=VMEM),
        cost_estimate=pl.CostEstimate(flops=count * full**3 * 12, bytes_accessed=count * full * full * 5, transcendentals=0),
        name="products",
    )(half, own, sent, got, got)


def local(group, traces):
    rows, size, nt = traces.shape
    flag = lax.axis_index("half").astype(jnp.int32).reshape(1)
    chunks = split(group)
    forward, inverse = make_tables(nt)
    table = forward.reshape(nt, 2 * F).T
    counts = [2 * group * n for n in chunks]
    spectra = transform(traces, jnp.asarray(table[: counts[0]]), counts[:1])
    spectra += transform(traces, jnp.asarray(table[counts[0] :]), counts[1:])
    parts = []
    for n, spectrum in zip(chunks, spectra):
        spectrum = spectrum.reshape(group, n, 2, rows, size)
        mine = lax.all_to_all(spectrum, "member", split_axis=0, concat_axis=0, tiled=True)
        own, sent = pack(flag, mine)
        got = lax.ppermute(sent, "half", [(0, 1), (1, 0)])
        predicted = products(flag, own, sent, got, group)
        returned = lax.all_to_all(predicted, "member", split_axis=0, concat_axis=0, tiled=True)
        parts.append(returned.reshape(group * n * 2, rows, size))
    return restore(parts, jnp.asarray(inverse.reshape(2 * F, nt)))


def solution(mesh):
    lines, count = mesh.shape["lines"], mesh.shape["tile"]
    group = count // 2
    inside = Mesh(mesh.devices.reshape(lines, 2, group), ("lines", "half", "member"))
    spec = P(inside.axis_names, None, None)

    def body(traces):
        return local(group, traces)

    return jax.shard_map(body, mesh=inside, in_specs=(spec,), out_specs=spec, check_vma=False)
```

```python
import math

import jax
import jax.numpy as jnp
import numpy as np
from jax import lax
from jax.experimental import pallas as pl
from jax.experimental.pallas import tpu as pltpu
from jax.sharding import Mesh
from jax.sharding import PartitionSpec as P

F = 128
VMEM = 60 << 20
SIZES = (3, 4, 5, 4, 16)


def make_tables(nt):
    times = np.arange(nt, dtype=np.int64)
    freqs = np.arange(F, dtype=np.int64)
    angle = ((times[:, None] * freqs[None, :]) % nt).astype(np.float32) * np.float32(2.0 * math.pi / nt)
    norm = np.float32(1.0 / math.sqrt(nt))
    forward = np.stack([np.cos(angle), -np.sin(angle)], axis=-1) * norm
    weight = np.where(freqs == 0, 1.0, 2.0).astype(np.float32)
    inverse = np.stack([np.cos(angle).T * weight[:, None], -np.sin(angle).T * weight[:, None]], axis=1) * norm
    return forward.astype(jnp.bfloat16), inverse.astype(jnp.bfloat16)


def split(group):
    share = F // group
    marks = [round(share * mark / SIZES[-1]) for mark in np.cumsum((0,) + SIZES[:-1])]
    return [b - a for a, b in zip(marks, marks[1:]) if b > a]


def grid_masks(size):
    row = lax.broadcasted_iota(jnp.int32, (size, size), 0)
    col = lax.broadcasted_iota(jnp.int32, (size, size), 1)
    return row, col


def forward_kernel(traces_ref, table_ref, *refs):
    outs, scratch = refs[:-1], refs[-1]
    rows = traces_ref.shape[0]
    count = table_ref.shape[0]
    for s in range(rows):
        value = lax.dot_general(
            table_ref[...], traces_ref[s], (((1,), (1,)), ((), ())), preferred_element_type=jnp.float32
        )
        for lane in range(scratch.shape[0]):
            scratch[lane, pl.ds(s, count, stride=rows), :] = value[:, lane * 128 : (lane + 1) * 128]
    at = 0
    for out in outs:
        n = out.shape[0]
        for lane in range(scratch.shape[0]):
            piece = scratch[lane, at * rows : (at + n) * rows, :].reshape(n, rows, 128)
            out[:, :, lane * 128 : (lane + 1) * 128] = piece.astype(jnp.bfloat16)
        at += n


def inverse_kernel(*refs):
    ins, table_ref, out_ref, scratch = refs[:-3], refs[-3], refs[-2], refs[-1]
    rows = out_ref.shape[0]
    count = table_ref.shape[0]
    at = 0
    for ref in ins:
        n = ref.shape[0]
        for lane in range(scratch.shape[0]):
            piece = ref[:, :, lane * 128 : (lane + 1) * 128].astype(jnp.float32)
            scratch[lane, at * rows : (at + n) * rows, :] = piece.reshape(n * rows, 128)
        at += n
    for s in range(rows):
        lanes = [scratch[lane, pl.ds(s, count, stride=rows), :] for lane in range(scratch.shape[0])]
        value = jnp.concatenate(lanes, axis=1).T.astype(jnp.bfloat16)
        out_ref[s] = jnp.dot(value, table_ref[...], preferred_element_type=jnp.float32).astype(jnp.bfloat16)


def transform(traces, table, counts):
    rows, size, nt = traces.shape
    total = table.shape[0]
    block = min(rows, 16)
    lanes = min(size, 256)
    return pl.pallas_call(
        forward_kernel,
        out_shape=tuple(jax.ShapeDtypeStruct((n, rows, size), jnp.bfloat16) for n in counts),
        grid=(rows // block, size // lanes),
        in_specs=[
            pl.BlockSpec((block, lanes, nt), lambda i, j: (i, j, 0)),
            pl.BlockSpec((total, nt), lambda i, j: (0, 0)),
        ],
        out_specs=tuple(pl.BlockSpec((n, block, lanes), lambda i, j: (0, i, j)) for n in counts),
        scratch_shapes=[pltpu.VMEM((lanes // 128, total * block, 128), jnp.float32)],
        compiler_params=pltpu.CompilerParams(vmem_limit_bytes=VMEM),
        cost_estimate=pl.CostEstimate(
            flops=2 * rows * size * nt * total, bytes_accessed=2 * rows * size * (nt + total), transcendentals=0
        ),
        name="transform",
    )(traces, table)


def restore(parts, table):
    rows, size = parts[0].shape[1:]
    total, nt = table.shape
    block = min(rows, 16)
    lanes = min(size, 256)
    return pl.pallas_call(
        inverse_kernel,
        out_shape=jax.ShapeDtypeStruct((rows, size, nt), jnp.bfloat16),
        grid=(rows // block, size // lanes),
        in_specs=[pl.BlockSpec((p.shape[0], block, lanes), lambda i, j: (0, i, j)) for p in parts]
        + [pl.BlockSpec((total, nt), lambda i, j: (0, 0))],
        out_specs=pl.BlockSpec((block, lanes, nt), lambda i, j: (i, j, 0)),
        scratch_shapes=[pltpu.VMEM((lanes // 128, total * block, 128), jnp.float32)],
        compiler_params=pltpu.CompilerParams(vmem_limit_bytes=VMEM),
        cost_estimate=pl.CostEstimate(
            flops=2 * rows * size * nt * total, bytes_accessed=2 * rows * size * (nt + total), transcendentals=0
        ),
        name="restore",
    )(*parts, table)


def pack_kernel(half_ref, mine_ref, own_ref, sent_ref):
    size = own_ref.shape[2]
    half = half_ref[0]
    near = pl.multiple_of(half * size, size)
    far = pl.multiple_of((1 - half) * size, size)
    own = []
    for c in range(2):
        block = mine_ref[:, 0, c, :, pl.ds(near, size)].reshape(size, size).astype(jnp.float32)
        own.append(((block + block.T) * 0.5).astype(jnp.bfloat16))
        own_ref[0, c] = own[c]
        sent_ref[0, c * size : (c + 1) * size] = mine_ref[:, 0, c, :, pl.ds(far, size)].reshape(size, size)
    row, col = grid_masks(size)
    real, imag = own[0].astype(jnp.float32), own[1].astype(jnp.float32)
    sent_ref[0, 2 * size : 3 * size] = jnp.where(row <= col, real, imag).astype(jnp.bfloat16)
    diagonal = jnp.sum(jnp.where(row == col, imag, 0.0), axis=0, keepdims=True)
    tail = sent_ref.shape[1] - 3 * size
    sent_ref[0, 3 * size :] = jnp.broadcast_to(diagonal, (tail, size)).astype(jnp.bfloat16)


def product_kernel(half_ref, own_ref, sent_ref, got_ref, out_ref, lhs_ref, rhs_ref, sum_ref):
    group, rows, full = out_ref.shape[0], out_ref.shape[3], out_ref.shape[4]
    size = full // 2
    eta = 1.0 / math.sqrt(full)
    half = half_ref[0]
    near = pl.multiple_of(half * size, size)
    far = pl.multiple_of((1 - half) * size, size)
    row, col = grid_masks(size)
    packed = got_ref[0, 2 * size : 3 * size].astype(jnp.float32)
    turned = packed.T
    diagonal = got_ref[0, 3 * size :].astype(jnp.float32)[0:1]
    there = (
        jnp.where(row <= col, packed, turned),
        jnp.where(row > col, packed, jnp.where(row < col, turned, diagonal)),
    )
    for c in range(2):
        at = slice(c * size, (c + 1) * size)
        mixed = (sent_ref[0, at].astype(jnp.float32) + got_ref[0, at].astype(jnp.float32).T) * 0.5
        mixed = mixed.astype(jnp.bfloat16)
        turned = mixed.astype(jnp.float32).T.astype(jnp.bfloat16)
        base = c * full
        rhs_ref[base : base + size, 0:size] = own_ref[0, c]
        rhs_ref[base : base + size, size:full] = mixed
        rhs_ref[base + size : base + full, 0:size] = turned
        rhs_ref[base + size : base + full, size:full] = there[c].astype(jnp.bfloat16)
    lhs_ref[0:full, 0:full] = rhs_ref[0:full]
    lhs_ref[full:, full:] = rhs_ref[0:full]
    lhs_ref[full:, 0:full] = rhs_ref[full:]
    lhs_ref[0:full, full:] = -rhs_ref[full:]

    @pl.loop(0, 4)
    def _(step):
        at = pl.ds(pl.multiple_of(step * size, size), size)
        square = jnp.dot(lhs_ref[at, :], rhs_ref[...], preferred_element_type=jnp.float32)
        sum_ref[at, :] = (rhs_ref[at, :].astype(jnp.float32) + eta * square).astype(jnp.bfloat16)

    for c in range(2):
        value = jnp.dot(lhs_ref[c * full : c * full + size], sum_ref[...], preferred_element_type=jnp.float32)
        value = (eta * value).astype(jnp.bfloat16).reshape(group, rows, full)
        out_ref[:, 0, c, :, pl.ds(near, size)] = value[:, :, 0:size]
        out_ref[:, 0, c, :, pl.ds(far, size)] = value[:, :, size:full]


def pack(half, mine):
    group, count, _, rows, full = mine.shape
    size = full // 2
    sent = 3 * size + 16
    return pl.pallas_call(
        pack_kernel,
        out_shape=(
            jax.ShapeDtypeStruct((count, 2, size, size), jnp.bfloat16),
            jax.ShapeDtypeStruct((count, sent, size), jnp.bfloat16),
        ),
        grid_spec=pltpu.PrefetchScalarGridSpec(
            num_scalar_prefetch=1,
            grid=(count,),
            in_specs=[pl.BlockSpec((group, 1, 2, rows, full), lambda k, h: (0, k, 0, 0, 0))],
            out_specs=[
                pl.BlockSpec((1, 2, size, size), lambda k, h: (k, 0, 0, 0)),
                pl.BlockSpec((1, sent, size), lambda k, h: (k, 0, 0)),
            ],
        ),
        compiler_params=pltpu.CompilerParams(vmem_limit_bytes=VMEM),
        cost_estimate=pl.CostEstimate(flops=count * size * size * 8, bytes_accessed=count * full * full * 5, transcendentals=0),
        name="pack",
    )(half, mine)


def products(half, own, sent, got, group):
    count, size = own.shape[0], own.shape[2]
    full = 2 * size
    rows = size // group
    shape = jax.ShapeDtypeStruct((group, count, 2, rows, full), jnp.bfloat16)
    passed = pl.BlockSpec((1,) + got.shape[1:], lambda k, h: (k, 0, 0))
    return pl.pallas_call(
        product_kernel,
        out_shape=shape,
        grid_spec=pltpu.PrefetchScalarGridSpec(
            num_scalar_prefetch=1,
            grid=(count,),
            in_specs=[pl.BlockSpec((1, 2, size, size), lambda k, h: (k, 0, 0, 0)), passed, passed],
            out_specs=pl.BlockSpec((group, 1, 2, rows, full), lambda k, h: (0, k, 0, 0, 0)),
            scratch_shapes=[
                pltpu.VMEM((2 * full, 2 * full), jnp.bfloat16),
                pltpu.VMEM((2 * full, full), jnp.bfloat16),
                pltpu.VMEM((2 * full, full), jnp.bfloat16),
            ],
        ),
        compiler_params=pltpu.CompilerParams(vmem_limit_bytes=VMEM),
        cost_estimate=pl.CostEstimate(flops=count * full**3 * 12, bytes_accessed=count * full * full * 5, transcendentals=0),
        name="products",
    )(half, own, sent, got)


def local(group, traces):
    rows, size, nt = traces.shape
    flag = lax.axis_index("half").astype(jnp.int32).reshape(1)
    chunks = split(group)
    forward, inverse = make_tables(nt)
    table = forward.reshape(nt, 2 * F).T
    counts = [2 * group * n for n in chunks]
    spectra = transform(traces, jnp.asarray(table[: counts[0]]), counts[:1])
    spectra += transform(traces, jnp.asarray(table[counts[0] :]), counts[1:])
    parts = []
    for n, spectrum in zip(chunks, spectra):
        spectrum = spectrum.reshape(group, n, 2, rows, size)
        mine = lax.all_to_all(spectrum, "member", split_axis=0, concat_axis=0, tiled=True)
        own, sent = pack(flag, mine)
        got = lax.ppermute(sent, "half", [(0, 1), (1, 0)])
        predicted = products(flag, own, sent, got, group)
        returned = lax.all_to_all(predicted, "member", split_axis=0, concat_axis=0, tiled=True)
        parts.append(returned.reshape(group * n * 2, rows, size))
    return restore(parts, jnp.asarray(inverse.reshape(2 * F, nt)))


def solution(mesh):
    lines, count = mesh.shape["lines"], mesh.shape["tile"]
    group = count // 2
    inside = Mesh(mesh.devices.reshape(lines, 2, group), ("lines", "half", "member"))
    spec = P(inside.axis_names, None, None)

    def body(traces):
        return local(group, traces)

    return jax.shard_map(body, mesh=inside, in_specs=(spec,), out_specs=spec, check_vma=False)
```
